32 devices in a mesh: gx: 4 (over y, core), gy: 8 (over z, x).
Axes of the slice: x: 2, y: 2, z: 4, core: 2. Of those that a mesh axis runs over, the one named last changes fastest.
Arguments:
- tokens: bfloat16 [4, 256, 6144], P('gx', None, 'gy'), may hold values from -6 to 6
- norm_gain: float32 [6144], replicated, may hold values from 0.1 to 1.9
- qkv_weight: bfloat16 [6144, 3, 4096], P('gx', None, 'gy'), may hold values from -0.078125 to 0.078125
- up_weight: bfloat16 [6144, 24576], P('gx', 'gy'), may hold values from -0.078125 to 0.078125
- query_gain: float32 [128], replicated, may hold values from 0.1 to 1.9
- key_gain: float32 [128], replicated, may hold values from 0.1 to 1.9
- out_weight: bfloat16 [4096, 6144], P('gy', 'gx'), may hold values from -0.09375 to 0.09375
- down_weight: bfloat16 [24576, 6144], P('gy', 'gx'), may hold values from -0.0390625 to 0.0390625
- attention_keep: int32 [4, 256, 6144], P('gx', None, 'gy'), may hold values 0 or 1
- feedforward_keep: int32 [4, 256, 6144], P('gx', None, 'gy'), may hold values 0 or 1
Outputs:
- block_out: bfloat16 [4, 256, 6144], P('gx', None, 'gy')
The draws below stay inside these ranges and needn't reach their ends.
All inputs are finite; a program needn't handle non-finite values. No bound on the sum of `attention_keep` or of `feedforward_keep` on one device may be relied on, other than what follows from the above.
Results may differ from the reference program's by a relative error of at most 0.017.
Values may be sent and summed in bfloat16 or wider, within the bound.
A program may use at most 128 MiB of HBM per device.

```python
import jax
import jax.numpy as jnp
from jax import lax

D = 6144
HEADS = 32
HDIM = 128
FF = 24576
SEQ = 256
IMAGES = 4
INNER = 4096
N_GX = 4
N_GY = 8


def place_ends(entries, key, low, top_value):
    longest = entries.shape.index(max(entries.shape))
    spots = []
    for shift in (0, 1):
        where = [jax.random.randint(jax.random.fold_in(key, axis), (), 0, length) for axis, length in enumerate(entries.shape)]
        where[longest] = (where[longest] + shift) % entries.shape[longest]
        spots.append(tuple(where))
    return entries.at[spots[0]].set(low).at[spots[1]].set(top_value)


def steps_of(stream_key, dims, split, low, largest):
    level, own = 1.0, jax.random.fold_in(stream_key, 6)
    for dim, shards_of in split:
        steps = jnp.exp(jax.random.uniform(jax.random.fold_in(own, dim), (shards_of,), jnp.float32, low / len(split), largest / len(split)))
        level = level * jnp.repeat(steps, dims[dim] // shards_of).reshape([-1 if axis == dim else 1 for axis in range(len(dims))])
    return level


def scatter_about(rng, extent, spread, limit, cuts=(), kind=jnp.bfloat16):
    values = spread * jax.random.normal(rng, extent, jnp.float32)
    if cuts:
        values = values * steps_of(rng, extent, cuts, -0.22, 0.18)
    return jnp.clip(values, -limit, limit).astype(kind)


def setup_inputs(seed: int = 0) -> dict:
    key_of = jax.random.split(jax.random.key(seed), 11)
    return {
        "tokens": scatter_about(key_of[0], (IMAGES, SEQ, D), 1.0, 6.0, ((0, 4), (2, 8))),
        "norm_gain": jnp.clip(1.0 + 0.18 * jax.random.normal(key_of[1], (D,), jnp.float32), 0.1, 1.9),
        "qkv_weight": scatter_about(key_of[2], (D, 3, INNER), D ** -0.5, 0.078125, ((0, 4), (2, 8))),
        "up_weight": scatter_about(key_of[3], (D, FF), D ** -0.5, 0.078125, ((0, 4), (1, 8))),
        "query_gain": jnp.clip(1.0 + 0.18 * jax.random.normal(key_of[4], (HDIM,), jnp.float32), 0.1, 1.9),
        "key_gain": jnp.clip(1.0 + 0.18 * jax.random.normal(key_of[5], (HDIM,), jnp.float32), 0.1, 1.9),
        "out_weight": scatter_about(key_of[6], (INNER, D), INNER ** -0.5, 0.09375, ((0, 8), (1, 4))),
        "down_weight": scatter_about(key_of[7], (FF, D), FF ** -0.5, 0.0390625, ((0, 8), (1, 4))),
        "attention_keep": place_ends((jax.random.randint(key_of[8], (IMAGES, SEQ, D), 0, 10) < 9).astype(jnp.int32), jax.random.fold_in(key_of[8], 1), 0, 1),
        "feedforward_keep": place_ends((jax.random.randint(key_of[9], (IMAGES, SEQ, D), 0, 10) < 9).astype(jnp.int32), jax.random.fold_in(key_of[9], 1), 0, 1),
    }


epsilon = 1e-06
keep_scale = 1.0 / 0.9

def layer_norm(values, gain):
    center = values - lax.optimization_barrier(jnp.mean(values, axis=-1, keepdims=True))
    variance = lax.optimization_barrier(jnp.mean(center * center, axis=-1, keepdims=True))
    return center * lax.rsqrt(variance + epsilon) * gain

def head_norm(values, gain):
    row_count = values.shape[0]
    shaped = values.reshape(row_count, -1, gain.shape[0])
    return layer_norm(shaped, gain).reshape(row_count, -1)

def rounded_sum(left, right, block_width, count):

    def accumulate(running, index):
        offset = index * block_width
        segment = lax.dynamic_slice_in_dim(left, offset, block_width, 1)
        rows_part = lax.dynamic_slice_in_dim(right, offset, block_width, 0)
        term = jnp.dot(segment, rows_part, preferred_element_type=jnp.float32).astype(jnp.bfloat16)
        term = lax.optimization_barrier(term)
        return (running + term.astype(jnp.float32), None)
    begin = jnp.zeros((left.shape[0], right.shape[1]), jnp.float32)
    total, unused = lax.scan(accumulate, begin, jnp.arange(count, dtype=jnp.int32))
    return total

def reference(tokens, norm_gain, qkv_weight, up_weight, query_gain, key_gain, out_weight, down_weight, attention_keep, feedforward_keep):
    row_total = IMAGES * SEQ
    inner = HEADS * HDIM
    normed = layer_norm(tokens.astype(jnp.float32), norm_gain).astype(jnp.bfloat16).reshape(row_total, D)
    joined = jnp.concatenate([qkv_weight.reshape(D, 3 * inner), up_weight], axis=1)
    united = rounded_sum(normed, joined, D // N_GX, N_GX)
    queries = head_norm(united[:, :inner], query_gain).astype(jnp.bfloat16)
    keys = head_norm(united[:, inner:2 * inner], key_gain).astype(jnp.bfloat16)
    values = united[:, 2 * inner:3 * inner].astype(jnp.bfloat16)
    query_grid = queries.reshape(IMAGES, SEQ, HEADS, HDIM).astype(jnp.float32)
    key_grid = keys.reshape(IMAGES, SEQ, HEADS, HDIM).astype(jnp.float32)
    value_grid = values.reshape(IMAGES, SEQ, HEADS, HDIM).astype(jnp.float32)
    scores = jnp.einsum('bshd,bthd->bhst', query_grid, key_grid) * HDIM ** (-0.5)
    raised = jnp.exp(scores)
    weights = (raised / lax.optimization_barrier(jnp.sum(raised, axis=-1, keepdims=True))).astype(jnp.bfloat16)
    attended = jnp.einsum('bhst,bthd->bshd', weights.astype(jnp.float32), value_grid)
    attended = attended.astype(jnp.bfloat16).reshape(row_total, inner)
    hidden = jax.nn.gelu(united[:, 3 * inner:], approximate=False).astype(jnp.bfloat16)
    attention_out = rounded_sum(attended, out_weight, inner // N_GY, N_GY).reshape(IMAGES, SEQ, D)
    feedforward_out = rounded_sum(hidden, down_weight, FF // N_GY, N_GY).reshape(IMAGES, SEQ, D)
    branches = attention_keep.astype(jnp.float32) * attention_out + feedforward_keep.astype(jnp.float32) * feedforward_out
    return (tokens.astype(jnp.float32) + branches * keep_scale).astype(jnp.bfloat16)
```

```python
import jax
import jax.numpy as jnp
from jax import lax
from jax.sharding import PartitionSpec as P

epsilon = 1e-06
keep_scale = 1.0 / 0.9
UP_CHUNKS = 2

f32 = jnp.float32
bf16 = jnp.bfloat16


def layer_norm(values, gain):
    center = values - jnp.mean(values, axis=-1, keepdims=True)
    variance = jnp.mean(center * center, axis=-1, keepdims=True)
    return center * lax.rsqrt(variance + epsilon) * gain


def head_norm(values, gain):
    row_count = values.shape[0]
    shaped = values.reshape(row_count, -1, gain.shape[0])
    return layer_norm(shaped, gain).reshape(row_count, -1)


def mul(left, right):
    return jnp.dot(left, right, preferred_element_type=f32)


def swap(values, bit, n_gx):
    return lax.ppermute(values, "gx", [(i, i ^ bit) for i in range(n_gx)])


def scatter_sum(odd_rows, even_rows, weight, n_gx):
    received = swap(mul(odd_rows, weight).astype(bf16), 1, n_gx)
    total = mul(even_rows, weight).astype(bf16).astype(f32) + received.astype(f32)
    bit, width = 2, weight.shape[1]
    own_rows = 2 * odd_rows.shape[0] // n_gx
    while bit < n_gx:
        pairs = total.reshape(-1, 2, own_rows, width)
        received = swap(pairs[:, 1].astype(bf16), bit, n_gx)
        total = pairs[:, 0] + received.astype(f32)
        bit *= 2
    return total.reshape(own_rows, width)


def gather_pair(own, n_gx):
    held, bit = own, n_gx // 2
    while bit > 1:
        held = jnp.concatenate([held, swap(held, bit, n_gx)], axis=0)
        bit //= 2
    return held, swap(held, 1, n_gx)


def gather_order(n_gx):
    order, bit = [0], n_gx // 2
    while bit >= 1:
        order = order + [p ^ bit for p in order]
        bit //= 2
    return order


def ring_place(index, count):
    return jnp.where(index % 2 == 0, index // 2, count - 1 - index // 2)


def ring_gather(own, ring, place):
    n = len(ring)
    ahead = [(ring[r], ring[(r + 1) % n]) for r in range(n)]
    back = [(b, a) for a, b in ahead]
    forward, backward = [own], [own]
    for step in range(n // 2 - 1):
        forward.append(lax.ppermute(forward[-1], "gy", ahead))
        backward.append(lax.ppermute(backward[-1], "gy", back))
    half = own.shape[0] // 2
    far = jnp.concatenate(
        [
            lax.ppermute(forward[-1][:half], "gy", ahead),
            lax.ppermute(backward[-1][half:], "gy", back),
        ],
        axis=0,
    )
    return jnp.stack(forward + [far] + backward[:0:-1])


def ring_scatter(partial, ring, place):
    n = len(ring)
    half = partial.shape[1] // 2
    ahead = [(ring[r], ring[(r + 1) % n]) for r in range(n)]
    back = [(b, a) for a, b in ahead]

    def block(index, start):
        index = lax.rem(index + 2 * n, n)
        return lax.dynamic_slice(
            partial, (index, start, 0), (1, half, partial.shape[2])
        )[0]

    up, down = block(place - 1, 0), block(place + 1, half)
    for step in range(n - 1):
        came_up = lax.ppermute(up, "gy", ahead)
        came_down = lax.ppermute(down, "gy", back)
        up = came_up.astype(f32) + block(place - 2 - step, 0).astype(f32)
        down = came_down.astype(f32) + block(place + 2 + step, half).astype(f32)
        up, down = up.astype(bf16), down.astype(bf16)
    return jnp.concatenate([up, down], axis=0)


def per_device(
    tokens,
    norm_gain,
    qkv_weight,
    up_weight,
    query_gain,
    key_gain,
    out_weight,
    down_weight,
    attention_keep,
    feedforward_keep,
):
    n_gx, n_gy = lax.axis_size("gx"), lax.axis_size("gy")
    sub = n_gy // n_gx
    me = lax.axis_index("gx")
    ring = list(range(0, n_gy, 2)) + list(range(1, n_gy, 2))[::-1]
    place = ring_place(lax.axis_index("gy"), n_gy)
    images, seq_len, slice_width = tokens.shape
    own_rows = images * seq_len
    block_width = qkv_weight.shape[0]
    head_cols = qkv_weight.shape[2]
    head_size = query_gain.shape[0]

    flat = tokens.reshape(own_rows, slice_width)
    turned = lax.ppermute(
        flat,
        ("gx", "gy"),
        [
            (i * n_gy + k * sub + s, k * n_gy + i * sub + s)
            for i in range(n_gx)
            for k in range(n_gx)
            for s in range(sub)
        ],
    )
    gathered = ring_gather(turned, ring, place)

    wide = flat.astype(f32)
    mean = jnp.mean(wide, axis=1)
    squares = jnp.sum((wide - mean[:, None]) ** 2, axis=1)
    count, bit = slice_width, 1
    while bit < n_gy:
        pairs = [(i, i ^ bit) for i in range(n_gy)]
        other = lax.ppermute(jnp.stack([mean, squares]), "gy", pairs)
        squares = squares + other[1] + (0.5 * count) * (mean - other[0]) ** 2
        mean = 0.5 * (mean + other[0])
        count, bit = 2 * count, 2 * bit
    stats = jnp.stack([mean, lax.rsqrt(squares / count + epsilon)])[None]
    bit = 1
    while bit < n_gx:
        stats = jnp.concatenate([stats, swap(stats, bit, n_gx)], axis=0)
        bit *= 2
    gain = lax.dynamic_slice_in_dim(norm_gain, me * block_width, block_width, 0)

    def normed_rows(position):
        image = me ^ position
        rows = jnp.concatenate(
            [
                lax.dynamic_index_in_dim(
                    gathered,
                    lax.rem(place - ring_place(image * sub + s, n_gy) + n_gy, n_gy),
                    0,
                    keepdims=False,
                )
                for s in range(sub)
            ],
            axis=1,
        ).astype(f32)
        row_mean, row_scale = stats[position, 0], stats[position, 1]
        return ((rows - row_mean[:, None]) * row_scale[:, None] * gain).astype(bf16)

    odd_rows = jnp.concatenate([normed_rows(p) for p in range(1, n_gx, 2)], axis=0)
    even_rows = jnp.concatenate([normed_rows(p) for p in range(0, n_gx, 2)], axis=0)

    qkv_flat = qkv_weight.reshape(block_width, 3 * head_cols)
    united = scatter_sum(odd_rows, even_rows, qkv_flat, n_gx)
    up_cols = up_weight.shape[1] // UP_CHUNKS
    hidden = []
    for c in range(UP_CHUNKS):
        total = scatter_sum(
            odd_rows, even_rows, up_weight[:, c * up_cols : (c + 1) * up_cols], n_gx
        )
        hidden.append(jax.nn.gelu(total, approximate=False).astype(bf16))

    queries = head_norm(united[:, :head_cols], query_gain).astype(bf16)
    keys = head_norm(united[:, head_cols : 2 * head_cols], key_gain).astype(bf16)
    values = united[:, 2 * head_cols :].astype(bf16)
    query_grid = queries.reshape(images, seq_len, -1, head_size)
    key_grid = keys.reshape(images, seq_len, -1, head_size)
    value_grid = values.reshape(images, seq_len, -1, head_size)
    scores = jnp.einsum(
        "bshd,bthd->bhst", query_grid, key_grid, preferred_element_type=f32
    ) * head_size ** (-0.5)
    raised = jnp.exp(scores)
    weights = (raised / jnp.sum(raised, axis=-1, keepdims=True)).astype(bf16)
    attended = jnp.einsum("bhst,bthd->bshd", weights, value_grid, preferred_element_type=f32)
    attended = attended.astype(bf16).reshape(own_rows, head_cols)

    order = gather_order(n_gx)
    def home(devices):
        return [
            (
                k * n_gy + devices[s * n_gx + q],
                (k ^ order[q]) * n_gy + k * sub + s,
            )
            for k in range(n_gx)
            for s in range(sub)
            for q in range(n_gx)
        ]

    def columns(weight, s):
        return weight[:, s * slice_width : (s + 1) * slice_width]

    attended_halves = gather_pair(attended, n_gx)
    attention_out = lax.psum_scatter(
        jnp.concatenate(
            [
                mul(rows, columns(out_weight, s)).astype(bf16)
                for s in range(sub)
                for rows in attended_halves
            ],
            axis=0,
        ),
        "gy",
        scatter_dimension=0,
        tiled=True,
    )
    attention_out = lax.ppermute(attention_out, ("gx", "gy"), home(range(n_gy))).astype(f32)
    hidden_halves = [gather_pair(part, n_gx) for part in hidden]
    pieces = []
    for s in range(sub):
        for half in range(2):
            total = 0.0
            for c in range(UP_CHUNKS):
                weight = down_weight[c * up_cols : (c + 1) * up_cols]
                total = total + mul(hidden_halves[c][half], columns(weight, s))
            pieces.append(total.astype(bf16))
    partial = jnp.concatenate(pieces, axis=0).reshape(n_gy, own_rows, slice_width)
    feedforward_out = ring_scatter(partial, ring, place)
    feedforward_out = lax.ppermute(feedforward_out, ("gx", "gy"), home(ring)).astype(f32)

    shape = tokens.shape
    branches = attention_keep.astype(f32) * attention_out.reshape(
        shape
    ) + feedforward_keep.astype(f32) * feedforward_out.reshape(shape)
    return (tokens.astype(f32) + branches * keep_scale).astype(bf16)


def solution(mesh):
    in_specs = (
        P("gx", None, "gy"),
        P(),
        P("gx", None, "gy"),
        P("gx", "gy"),
        P(),
        P(),
        P("gy", "gx"),
        P("gy", "gx"),
        P("gx", None, "gy"),
        P("gx", None, "gy"),
    )
    out_specs = P("gx", None, "gy")
    return jax.shard_map(
        per_device, mesh=mesh, in_specs=in_specs, out_specs=out_specs, check_vma=False
    )
```
